32 devices in a mesh: seg: 4 (over y, x), chan: 8 (over z, core).
Axes of the slice: x: 2, y: 2, z: 4, core: 2. Of those that a mesh axis runs over, the one named last changes fastest.
Arguments:
- record: bfloat16 [1280, 16384], P('chan', 'seg'), may hold values from -6 to 6
- valid: int32 [1280], P('chan'), may hold values 0 or 1
- pairs: int32 [2, 8], P(None, 'chan'), may hold values from 0 to 7
Outputs:
- cross: bfloat16 [2, 2, 200, 204800], P(None, None, 'seg', 'chan')
The draws below stay inside these ranges and needn't reach their ends.
All inputs are finite; a program needn't handle non-finite values. No bound on the sum of `valid` on one device may be relied on, other than what follows from the above.
Results may differ from the reference program's by a relative error of at most 0.008.
Values may be sent and summed in bfloat16 or wider, within the bound.
A program may use at most 128 MiB of HBM per device.

```python
import math
import jax
import jax.numpy as jnp
from jax import lax

BLK_CH = 160
FREQS = 200
WIN = 1024
LOW_BIN = 24
STEPS = 2
BAND = 3
HOP = 512
SEGLEN = 4096
NT = 16384
NBLK = 8
NCH = 1280
N_SEG = 4


def draw_pairs(key, part):
    first_key, second_key = jax.random.split(jax.random.fold_in(key, 11))
    distance = jax.random.randint(first_key, (STEPS, NBLK), 1, BAND + 1)
    direction = 2 * jax.random.randint(second_key, (STEPS, NBLK), 0, 2) - 1
    blocks = jnp.arange(NBLK, dtype=jnp.int32)[None, :]
    forward = blocks + direction * distance
    inside = (forward >= 0) & (forward < NBLK)
    partner = jnp.where(inside, forward, blocks - direction * distance)
    partner = partner.at[0, 0].set(BAND)
    partner = partner.at[0, NBLK - 1].set(NBLK - 1 - BAND)
    for reach_k in range(1, BAND + 1):
        partner = partner.at[1, reach_k].set(0)
        partner = partner.at[1, NBLK - 1 - reach_k].set(NBLK - 1)
    return partner.astype(jnp.int32)


def plant(entries, own_key, low, top_value):
    longest = entries.shape.index(max(entries.shape))
    spots = []
    for shift in (0, 1):
        where = [jax.random.randint(jax.random.fold_in(own_key, axis), (), 0, length) for axis, length in enumerate(entries.shape)]
        where[longest] = (where[longest] + shift) % entries.shape[longest]
        spots.append(tuple(where))
    return entries.at[spots[0]].set(low).at[spots[1]].set(top_value)


def block_levels(key, extent, cuts, low, high):
    level, own = 1.0, jax.random.fold_in(key, 6)
    for position, parts in cuts:
        heights = jnp.exp(jax.random.uniform(jax.random.fold_in(own, position), (parts,), jnp.float32, low / len(cuts), high / len(cuts)))
        level = level * jnp.repeat(heights, extent[position] // parts).reshape([-1 if axis == position else 1 for axis in range(len(extent))])
    return level


def centred(key, dims, spread, reach, pieces=(), held_as=jnp.bfloat16):
    gain = block_levels(key, dims, pieces, -0.22, 0.18) if pieces else 1.0
    result = jax.random.normal(key, dims, jnp.float32) * spread * gain
    return jnp.minimum(jnp.maximum(result, -reach), reach).astype(held_as)


def setup_inputs(seed: int = 0) -> dict:
    streams_of = jax.random.split(jax.random.key(seed), 4)
    record = centred(streams_of[0], (NCH, NT), 1.0, 6.0, ((0, 8), (1, 4)))
    valid = plant((jax.random.randint(streams_of[1], (NCH,), 0, 8) < 7).astype(jnp.int32), jax.random.fold_in(streams_of[1], 1), 0, 1)
    pairs = draw_pairs(jax.random.fold_in(streams_of[3], 71), 0)
    return dict(record=record, valid=valid, pairs=pairs)


def band_table():
    steps_k = jnp.arange(WIN, dtype=jnp.int32)
    bins = LOW_BIN + jnp.arange(FREQS, dtype=jnp.int32)
    phase = steps_k[:, None] * bins[None, :] % WIN
    angle = 2.0 * math.pi / WIN * phase.astype(jnp.float32)
    taper = 0.5 - 0.5 * jnp.cos(2.0 * math.pi / WIN * steps_k.astype(jnp.float32))
    factor = (8.0 / (3.0 * WIN)) ** 0.5
    cos_part = taper[:, None] * jnp.cos(angle) * factor
    sin_part = -taper[:, None] * jnp.sin(angle) * factor
    return jnp.stack([cos_part, sin_part], axis=1).astype(jnp.bfloat16)

def cross_gram(left, right, factor):
    real_part = jnp.einsum('wfi,wfj->fij', left[:, 0], right[:, 0]) + jnp.einsum('wfi,wfj->fij', left[:, 1], right[:, 1])
    imag_part = jnp.einsum('wfi,wfj->fij', left[:, 1], right[:, 0]) - jnp.einsum('wfi,wfj->fij', left[:, 0], right[:, 1])
    return (jnp.stack([real_part, imag_part], axis=0) * factor).astype(jnp.bfloat16)

def reference(record, valid, pairs):
    samples = record.astype(jnp.float32).reshape(NCH, N_SEG, SEGLEN)
    scale = jnp.sqrt(lax.optimization_barrier(jnp.mean(samples * samples, axis=-1, keepdims=True)) + 1e-05)
    normed = (samples / scale).astype(jnp.bfloat16).reshape(NCH, NT)
    padded = jnp.concatenate([normed, jnp.zeros((NCH, HOP), jnp.bfloat16)], axis=1)
    table = band_table().astype(jnp.float32)
    windows = NT // HOP
    usable = valid.astype(jnp.float32)

    def spectra_of(block):
        start = (block * BLK_CH).astype(jnp.int32)
        rows = lax.dynamic_slice_in_dim(padded, start, BLK_CH, 0)
        frames = jnp.concatenate([rows[:, :NT].reshape(BLK_CH, windows, HOP), rows[:, HOP:].reshape(BLK_CH, windows, HOP)], axis=-1)
        spec = jnp.einsum('cwk,kpf->wpfc', frames.astype(jnp.float32), table)
        mask_part = lax.dynamic_slice_in_dim(usable, start, BLK_CH, 0)
        return (spec * mask_part[None, None, None, :]).astype(jnp.bfloat16)
    spectra = lax.map(spectra_of, jnp.arange(NBLK, dtype=jnp.int32))
    factor = 1.0 / math.sqrt(windows)

    def pair_block(block):
        left = spectra[block].astype(jnp.float32)
        results = []
        for step in range(STEPS):
            right = spectra[pairs[step, block]].astype(jnp.float32)
            results.append(cross_gram(left, right, factor))
        return jnp.stack(results, axis=0)
    stacks = lax.map(pair_block, jnp.arange(NBLK, dtype=jnp.int32))
    stacks = jnp.transpose(stacks, (1, 2, 3, 0, 4, 5))
    return stacks.reshape(STEPS, 2, FREQS, NCH * BLK_CH)
```

```python
import functools
import math

import jax
import jax.numpy as jnp
from jax import lax
from jax.experimental import pallas as pl
from jax.experimental.pallas import tpu as pltpu
from jax.sharding import PartitionSpec as P

FREQS = 200
WIN = 1024
LOW_BIN = 24
STEPS = 2
BAND = 3
HOP = 512
GROUP = 8
LANES = 128


def shifted(value, axis, steps):
    count = lax.axis_size(axis)
    initial, last = (max(0, -steps), min(count, count - steps))
    return lax.ppermute(value, axis, [(source, source + steps) for source in range(initial, last)])


def band_table():
    steps_k = jnp.arange(WIN, dtype=jnp.int32)
    bins = LOW_BIN + jnp.arange(FREQS, dtype=jnp.int32)
    phase = steps_k[:, None] * bins[None, :] % WIN
    angle = 2.0 * math.pi / WIN * phase.astype(jnp.float32)
    taper = 0.5 - 0.5 * jnp.cos(2.0 * math.pi / WIN * steps_k.astype(jnp.float32))
    factor = (8.0 / (3.0 * WIN)) ** 0.5
    cos_part = taper[:, None] * jnp.cos(angle) * factor
    sin_part = -taper[:, None] * jnp.sin(angle) * factor
    return jnp.stack([cos_part, sin_part], axis=1).astype(jnp.bfloat16)


def gram_kernel(count, factor, sel_ref, own_ref, first_ref, second_ref, out_ref, low, high):
    del sel_ref
    group = pl.program_id(0)
    rows, chans = own_ref.shape[1:]
    half = rows // 2
    tail = chans - LANES

    def one_freq(f, carry):
        left = own_ref[f]
        for step, ref in enumerate((first_ref, second_ref)):
            right = ref[0, f]
            turned = jnp.concatenate([-right[half:], right[:half]], axis=0)
            for part, operand in enumerate((right, turned)):
                gram = lax.dot_general(
                    left, operand, (((0,), (0,)), ((), ())), preferred_element_type=jnp.float32
                )
                gram = gram * factor
                spot = 2 * step + part
                low[spot, pl.ds(f, chans, stride=GROUP), :] = gram[:, :LANES]
                rest = jnp.concatenate(
                    [gram[:, LANES:], jnp.zeros((chans, LANES - tail), jnp.float32)], axis=1
                )
                high[spot, pl.ds(f, chans, stride=GROUP), :] = rest
        return carry

    lax.fori_loop(0, jnp.minimum(GROUP, count - group * GROUP), one_freq, 0)
    batch = LANES // math.gcd(chans, LANES)

    def one_batch(a, carry):
        for spot in range(2 * STEPS):
            pieces = []
            for r in range(batch):
                at = pl.ds(pl.multiple_of((a * batch + r) * GROUP, GROUP), GROUP)
                pieces.append(low[spot, at, :])
                pieces.append(high[spot, at, :][:, :tail])
            merged = jnp.concatenate(pieces, axis=1).astype(jnp.bfloat16)
            width = batch * chans
            out_ref[spot // 2, spot % 2, :, pl.ds(pl.multiple_of(a * width, LANES), width)] = merged
        return carry

    lax.fori_loop(0, chans // batch, one_batch, 0)


def cross_stacks(own, stacked, chosen, factor):
    freqs, rows, chans = own.shape
    block = (1, GROUP, rows, chans)
    grid_spec = pltpu.PrefetchScalarGridSpec(
        num_scalar_prefetch=1,
        grid=(pl.cdiv(freqs, GROUP),),
        in_specs=[
            pl.BlockSpec((GROUP, rows, chans), lambda g, sel: (g, 0, 0)),
            pl.BlockSpec(block, lambda g, sel: (sel[0], g, 0, 0)),
            pl.BlockSpec(block, lambda g, sel: (sel[1], g, 0, 0)),
        ],
        out_specs=pl.BlockSpec((STEPS, 2, GROUP, chans * chans), lambda g, sel: (0, 0, g, 0)),
        scratch_shapes=[
            pltpu.VMEM((2 * STEPS, chans * GROUP, LANES), jnp.float32),
            pltpu.VMEM((2 * STEPS, chans * GROUP, LANES), jnp.float32),
        ],
    )
    return pl.pallas_call(
        functools.partial(gram_kernel, freqs, factor),
        grid_spec=grid_spec,
        out_shape=jax.ShapeDtypeStruct((STEPS, 2, freqs, chans * chans), jnp.bfloat16),
        compiler_params=pltpu.CompilerParams(vmem_limit_bytes=40 * 2**20),
        cost_estimate=pl.CostEstimate(
            flops=8 * STEPS * freqs * rows * chans * chans,
            bytes_accessed=4 * STEPS * freqs * chans * chans,
            transcendentals=0,
        ),
    )(chosen, own, stacked, stacked)


def fetch_band(spectra):
    above = []
    below = []
    for reach_k in range(1, BAND + 1):
        above.append(shifted(spectra, "chan", -reach_k))
        below.append(shifted(spectra, "chan", reach_k))
    return below[::-1] + above


def per_device(record, valid, pairs):
    channels, seg_len = record.shape
    windows = seg_len // HOP
    samples = record.astype(jnp.float32)
    scale = jnp.sqrt(jnp.mean(samples * samples, axis=-1, keepdims=True) + 1e-05)
    normed = (samples / scale).astype(jnp.bfloat16)
    following = shifted(normed[:, :HOP], "seg", -1)
    extended = jnp.concatenate([normed, following], axis=1)
    frames = jnp.concatenate(
        [
            extended[:, :seg_len].reshape(channels, windows, HOP),
            extended[:, HOP:].reshape(channels, windows, HOP),
        ],
        axis=-1,
    )
    spec = jnp.einsum("cwk,kpf->wpfc", frames, band_table(), preferred_element_type=jnp.float32)
    usable = valid.astype(jnp.float32)
    spectra = (spec * usable[None, None, None, :]).astype(jnp.bfloat16)
    got = lax.all_to_all(spectra, "seg", split_axis=2, concat_axis=0, tiled=True)
    total, _, freqs, _ = got.shape
    own = got.transpose(2, 1, 0, 3).reshape(freqs, 2 * total, channels)
    stacked = jnp.stack(fetch_band(own), axis=0)
    offset = pairs[:, 0] - lax.axis_index("chan")
    chosen = offset + BAND - (offset > 0).astype(jnp.int32)
    return cross_stacks(own, stacked, chosen, 1.0 / math.sqrt(total))


def solution(mesh):
    in_specs = (P("chan", "seg"), P("chan"), P(None, "chan"))
    out_specs = P(None, None, "seg", "chan")
    return jax.shard_map(
        per_device, mesh=mesh, in_specs=in_specs, out_specs=out_specs, check_vma=False
    )
```

```python
import functools
import math

import jax
import jax.numpy as jnp
from jax import lax
from jax.experimental import pallas as pl
from jax.experimental.pallas import tpu as pltpu
from jax.sharding import PartitionSpec as P

FREQS = 200
WIN = 1024
LOW_BIN = 24
STEPS = 2
BAND = 3
HOP = 512
LANES = 128


def shifted(value, axis, steps):
    count = lax.axis_size(axis)
    initial, last = (max(0, -steps), min(count, count - steps))
    return lax.ppermute(value, axis, [(source, source + steps) for source in range(initial, last)])


def band_table():
    steps_k = jnp.arange(WIN, dtype=jnp.int32)
    bins = LOW_BIN + jnp.arange(FREQS, dtype=jnp.int32)
    phase = steps_k[:, None] * bins[None, :] % WIN
    angle = 2.0 * math.pi / WIN * phase.astype(jnp.float32)
    taper = 0.5 - 0.5 * jnp.cos(2.0 * math.pi / WIN * steps_k.astype(jnp.float32))
    factor = (8.0 / (3.0 * WIN)) ** 0.5
    cos_part = taper[:, None] * jnp.cos(angle) * factor
    sin_part = -taper[:, None] * jnp.sin(angle) * factor
    return jnp.stack([cos_part, sin_part], axis=1).astype(jnp.bfloat16)


def gram_kernel(factor, sel_ref, own_ref, first_ref, second_ref, out_ref, *held):
    del sel_ref
    group, rows, _ = own_ref.shape
    chans = first_ref.shape[-1]
    batch = LANES // math.gcd(chans, LANES)
    reach = chans // batch
    width = batch * chans // LANES

    def one_freq(f, carry):
        left = own_ref[f]
        for step, ref in enumerate((first_ref, second_ref)):
            grams = jnp.dot(left, ref[0, f], preferred_element_type=jnp.float32)
            for part in range(2):
                pieces = []
                for r in range(batch):
                    at = (part * batch + r) * reach
                    pieces.append(grams[at : at + reach])
                for m in range(width):
                    parts = []
                    for r in range(batch):
                        low = max(m * LANES - r * chans, 0)
                        high = min((m + 1) * LANES - r * chans, chans)
                        if low < high:
                            parts.append(pieces[r][:, low:high])
                    line = parts[0] if len(parts) == 1 else jnp.concatenate(parts, axis=1)
                    held[step][pl.ds(2 * m + part, reach, stride=2 * width), :] = line
            out_ref[step, f] = (held[step][...] * factor).astype(jnp.bfloat16)
        return carry

    lax.fori_loop(0, group, one_freq, 0)


def gram_operand(own):
    freqs, rows, chans = own.shape
    half = rows // 2
    batch = LANES // math.gcd(chans, LANES)
    turned = jnp.concatenate([own[:, half:], -own[:, :half]], axis=1)
    both = jnp.stack([own, turned], axis=1).reshape(freqs, 2, rows, chans // batch, batch)
    return both.transpose(0, 1, 4, 3, 2).reshape(freqs, 2 * chans, rows)


def cross_stacks(own, stacked, chosen, factor):
    freqs, rows, chans = own.shape
    lines = 2 * chans * chans // LANES
    group = max(n for n in range(1, 9) if freqs % n == 0)
    block = (1, group, rows, chans)
    grid_spec = pltpu.PrefetchScalarGridSpec(
        num_scalar_prefetch=1,
        grid=(freqs // group,),
        in_specs=[
            pl.BlockSpec((group, 2 * chans, rows), lambda g, sel: (g, 0, 0)),
            pl.BlockSpec(block, lambda g, sel: (sel[0], g, 0, 0)),
            pl.BlockSpec(block, lambda g, sel: (sel[1], g, 0, 0)),
        ],
        out_specs=pl.BlockSpec((STEPS, group, lines, LANES), lambda g, sel: (0, g, 0, 0)),
        scratch_shapes=[pltpu.VMEM((lines, LANES), jnp.float32)] * STEPS,
    )
    merged = pl.pallas_call(
        functools.partial(gram_kernel, factor),
        grid_spec=grid_spec,
        out_shape=jax.ShapeDtypeStruct((STEPS, freqs, lines, LANES), jnp.bfloat16),
        compiler_params=pltpu.CompilerParams(vmem_limit_bytes=24 * 2**20),
        cost_estimate=pl.CostEstimate(
            flops=8 * STEPS * freqs * rows * chans * chans,
            bytes_accessed=4 * STEPS * freqs * chans * chans,
            transcendentals=0,
        ),
    )(chosen, gram_operand(own), stacked, stacked)
    merged = merged.reshape(STEPS, freqs, lines // 2, 2, LANES).transpose(0, 3, 1, 2, 4)
    return merged.reshape(STEPS, 2, freqs, chans * chans)


def fetch_band(spectra):
    above = []
    below = []
    for reach_k in range(1, BAND + 1):
        above.append(shifted(spectra, "chan", -reach_k))
        below.append(shifted(spectra, "chan", reach_k))
    return below[::-1] + above


def per_device(record, valid, pairs):
    channels, seg_len = record.shape
    windows = seg_len // HOP
    samples = record.astype(jnp.float32)
    scale = jnp.sqrt(jnp.mean(samples * samples, axis=-1, keepdims=True) + 1e-05)
    normed = (samples / scale).astype(jnp.bfloat16)
    following = shifted(normed[:, :HOP], "seg", -1)
    extended = jnp.concatenate([normed, following], axis=1)
    frames = jnp.concatenate(
        [
            extended[:, :seg_len].reshape(channels, windows, HOP),
            extended[:, HOP:].reshape(channels, windows, HOP),
        ],
        axis=-1,
    )
    spec = jnp.einsum("cwk,kpf->wpfc", frames, band_table(), preferred_element_type=jnp.float32)
    usable = valid.astype(jnp.float32)
    spectra = (spec * usable[None, None, None, :]).astype(jnp.bfloat16)
    got = lax.all_to_all(spectra, "seg", split_axis=2, concat_axis=0, tiled=True)
    total, _, freqs, _ = got.shape
    own = got.transpose(2, 1, 0, 3).reshape(freqs, 2 * total, channels)
    stacked = jnp.stack(fetch_band(own), axis=0)
    offset = pairs[:, 0] - lax.axis_index("chan")
    chosen = offset + BAND - (offset > 0).astype(jnp.int32)
    return cross_stacks(own, stacked, chosen, 1.0 / math.sqrt(total))


def solution(mesh):
    in_specs = (P("chan", "seg"), P("chan"), P(None, "chan"))
    out_specs = P(None, None, "seg", "chan")
    return jax.shard_map(
        per_device, mesh=mesh, in_specs=in_specs, out_specs=out_specs, check_vma=False
    )
```

```python
import functools
import math

import jax
import jax.numpy as jnp
from jax import lax
from jax.experimental import pallas as pl
from jax.experimental.pallas import tpu as pltpu
from jax.sharding import PartitionSpec as P

FREQS = 200
WIN = 1024
LOW_BIN = 24
STEPS = 2
BAND = 3
HOP = 512
LANES = 128


def shifted(value, axis, steps):
    count = lax.axis_size(axis)
    initial, last = (max(0, -steps), min(count, count - steps))
    return lax.ppermute(value, axis, [(source, source + steps) for source in range(initial, last)])


def band_table():
    steps_k = jnp.arange(WIN, dtype=jnp.int32)
    bins = LOW_BIN + jnp.arange(FREQS, dtype=jnp.int32)
    phase = steps_k[:, None] * bins[None, :] % WIN
    angle = 2.0 * math.pi / WIN * phase.astype(jnp.float32)
    taper = 0.5 - 0.5 * jnp.cos(2.0 * math.pi / WIN * steps_k.astype(jnp.float32))
    factor = (8.0 / (3.0 * WIN)) ** 0.5
    cos_part = taper[:, None] * jnp.cos(angle) * factor
    sin_part = -taper[:, None] * jnp.sin(angle) * factor
    return jnp.stack([cos_part, sin_part], axis=1).astype(jnp.bfloat16)


def gram_kernel(factor, sel_ref, own_ref, *refs):
    found, (out_ref, turn, held_a, held_b, partners, sems) = refs[:-6], refs[-6:]
    group, rows, wide = own_ref.shape
    chans = math.isqrt(out_ref.shape[2] * LANES // 2)
    batch = wide // chans
    half = rows // 2
    reach = chans // batch
    width = batch * chans // LANES
    start = pl.program_id(0) * group

    @pl.when(pl.program_id(0) == 0)
    def _():
        for step in range(STEPS):
            for place, ref in enumerate(found):

                @pl.when(sel_ref[step] == place)
                def _():
                    pltpu.make_async_copy(ref, partners.at[step], sems.at[step]).start()

        for step in range(STEPS):
            pltpu.make_async_copy(found[0], partners.at[step], sems.at[step]).wait()

    def one_freq(f, carry):
        own = own_ref[f].astype(jnp.float32)
        plain, turned = [], []
        for r in range(batch):
            piece = own[:, r * chans : (r + 1) * chans]
            plain.append(piece)
            turned += [piece[half:], -piece[:half]]
        upright = jnp.concatenate(plain + turned, axis=0).T
        columns = []
        for k in range(turn.shape[0]):
            turn[k] = upright[:, k * LANES : (k + 1) * LANES]
            columns.append(
                jnp.concatenate(
                    [turn[k, pl.ds(r, reach, stride=batch), :] for r in range(batch)], axis=0
                )
            )
        left = jnp.concatenate(columns, axis=1).astype(jnp.bfloat16)
        for step, held in enumerate((held_a, held_b)):
            packed = partners[step, start + f]
            right = jnp.concatenate(
                [packed[:, r * chans : (r + 1) * chans] for r in range(batch)], axis=0
            )
            empty = jnp.zeros_like(right)
            for part in range(2):
                operand = jnp.concatenate([empty, right] if part else [right, empty], axis=0)
                gram = jnp.dot(left, operand, preferred_element_type=jnp.float32)
                pieces = [gram[r * reach : (r + 1) * reach] for r in range(batch)]
                for m in range(width):
                    parts = []
                    for r in range(batch):
                        low = max(m * LANES - r * chans, 0)
                        high = min((m + 1) * LANES - r * chans, chans)
                        if low < high:
                            parts.append(pieces[r][:, low:high])
                    line = parts[0] if len(parts) == 1 else jnp.concatenate(parts, axis=1)
                    held[pl.ds(2 * m + part, reach, stride=2 * width), :] = line
            out_ref[step, f] = (held[...] * factor).astype(jnp.bfloat16)
        return carry

    lax.fori_loop(0, group, one_freq, 0)


def packed_windows(got, batch):
    total, _, freqs, chans = got.shape
    split = got.reshape(total // batch, batch, 2, freqs, chans)
    return split.transpose(3, 2, 0, 1, 4).reshape(freqs, 2 * total // batch, batch * chans)


def cross_stacks(own, found, chosen, chans, factor):
    freqs, rows, wide = own.shape
    double = 2 * rows * wide // chans
    lines = 2 * chans * chans // LANES
    group = max(n for n in range(1, 9) if freqs % n == 0)
    grid_spec = pltpu.PrefetchScalarGridSpec(
        num_scalar_prefetch=1,
        grid=(freqs // group,),
        in_specs=[pl.BlockSpec((group, rows, wide), lambda g, sel: (g, 0, 0))]
        + [pl.BlockSpec(memory_space=pl.ANY)] * len(found),
        out_specs=pl.BlockSpec((STEPS, group, lines, LANES), lambda g, sel: (0, g, 0, 0)),
        scratch_shapes=[pltpu.VMEM((double // LANES, chans, LANES), jnp.float32)]
        + [pltpu.VMEM((lines, LANES), jnp.float32)] * STEPS
        + [
            pltpu.VMEM((STEPS,) + found[0].shape, jnp.bfloat16),
            pltpu.SemaphoreType.DMA((STEPS,)),
        ],
    )
    merged = pl.pallas_call(
        functools.partial(gram_kernel, factor),
        grid_spec=grid_spec,
        out_shape=jax.ShapeDtypeStruct((STEPS, freqs, lines, LANES), jnp.bfloat16),
        compiler_params=pltpu.CompilerParams(vmem_limit_bytes=24 * 2**20),
        cost_estimate=pl.CostEstimate(
            flops=4 * STEPS * freqs * double * chans * chans,
            bytes_accessed=4 * STEPS * freqs * chans * chans,
            transcendentals=0,
        ),
    )(chosen, own, *found)
    merged = merged.reshape(STEPS, freqs, lines // 2, 2, LANES).transpose(0, 3, 1, 2, 4)
    return merged.reshape(STEPS, 2, freqs, chans * chans)


def fetch_band(own):
    count = lax.axis_size("chan")
    swap = [(b, b ^ 1) for b in range(count)]
    above = shifted(own, "chan", -2)
    below = shifted(own, "chan", 2)
    twin = lax.ppermute(own, "chan", swap)
    on_down = lax.ppermute(above, "chan", [(b, b - 1) for b in range(2, count, 2)])
    on_up = lax.ppermute(below, "chan", [(b, b + 1) for b in range(1, count - 1, 2)])
    twin_above = lax.ppermute(above, "chan", swap)
    twin_below = lax.ppermute(below, "chan", swap)
    return [twin, above, below, twin_above, twin_below, on_down, on_up]


PLACES = ((6, 2, 4, 0, 0, 1, 3), (4, 2, 0, 0, 3, 1, 5))


def per_device(record, valid, pairs):
    channels, seg_len = record.shape
    windows = seg_len // HOP
    samples = record.astype(jnp.float32)
    scale = jnp.sqrt(jnp.mean(samples * samples, axis=-1, keepdims=True) + 1e-05)
    normed = (samples / scale).astype(jnp.bfloat16)
    following = shifted(normed[:, :HOP], "seg", -1)
    extended = jnp.concatenate([normed, following], axis=1)
    frames = jnp.concatenate(
        [
            extended[:, :seg_len].reshape(channels, windows, HOP),
            extended[:, HOP:].reshape(channels, windows, HOP),
        ],
        axis=-1,
    )
    spec = jnp.einsum("cwk,kpf->wpfc", frames, band_table(), preferred_element_type=jnp.float32)
    usable = valid.astype(jnp.float32)
    spectra = (spec * usable[None, None, None, :]).astype(jnp.bfloat16)
    got = lax.all_to_all(spectra, "seg", split_axis=2, concat_axis=0, tiled=True)
    batch = LANES // math.gcd(channels, LANES)
    own = packed_windows(got, batch)
    found = fetch_band(own)
    block = lax.axis_index("chan")
    row = jnp.where(block % 2 == 1, jnp.array(PLACES[1]), jnp.array(PLACES[0]))
    chosen = row[pairs[:, 0] - block + BAND].astype(jnp.int32)
    return cross_stacks(own, found, chosen, channels, 1.0 / math.sqrt(got.shape[0]))


def solution(mesh):
    in_specs = (P("chan", "seg"), P("chan"), P(None, "chan"))
    out_specs = P(None, None, "seg", "chan")
    return jax.shard_map(
        per_device, mesh=mesh, in_specs=in_specs, out_specs=out_specs, check_vma=False
    )
```

```python
import functools
import math

import jax
import jax.numpy as jnp
from jax import lax
from jax.experimental import pallas as pl
from jax.experimental.pallas import tpu as pltpu
from jax.sharding import PartitionSpec as P

FREQS = 200
WIN = 1024
LOW_BIN = 24
STEPS = 2
BAND = 3
HOP = 512
LANES = 128


def shifted(value, axis, steps):
    count = lax.axis_size(axis)
    initial, last = (max(0, -steps), min(count, count - steps))
    return lax.ppermute(value, axis, [(source, source + steps) for source in range(initial, last)])


def band_table():
    steps_k = jnp.arange(WIN, dtype=jnp.int32)
    bins = LOW_BIN + jnp.arange(FREQS, dtype=jnp.int32)
    phase = steps_k[:, None] * bins[None, :] % WIN
    angle = 2.0 * math.pi / WIN * phase.astype(jnp.float32)
    taper = 0.5 - 0.5 * jnp.cos(2.0 * math.pi / WIN * steps_k.astype(jnp.float32))
    factor = (8.0 / (3.0 * WIN)) ** 0.5
    cos_part = taper[:, None] * jnp.cos(angle) * factor
    sin_part = -taper[:, None] * jnp.sin(angle) * factor
    return jnp.stack([cos_part, sin_part], axis=1).astype(jnp.bfloat16)


def turn_kernel(half, own_ref, left_ref, *turns):
    group, rows, wide = own_ref.shape
    chans = left_ref.shape[1]
    batch = wide // chans
    reach = chans // batch
    row = lax.broadcasted_iota(jnp.int32, (rows, chans), 0)
    real = row % (2 * half) < half
    for f in range(group):
        turn = turns[f]
        own = own_ref[f].astype(jnp.float32)
        plain = [own[:, r * chans : (r + 1) * chans] for r in range(batch)]
        turned = [
            jnp.where(real, pltpu.roll(p, rows - half, 0), -pltpu.roll(p, half, 0)) for p in plain
        ]
        upright = jnp.concatenate(plain + turned, axis=0).T
        for k in range(turn.shape[0]):
            turn[k] = upright[:, k * LANES : (k + 1) * LANES]
            for r in range(batch):
                left_ref[f, pl.ds(r * reach, reach), pl.ds(k * LANES, LANES)] = turn[
                    k, pl.ds(r, reach, stride=batch), :
                ].astype(jnp.bfloat16)


def turned_own(own, chans, half):
    freqs, rows, wide = own.shape
    double = 2 * rows * wide // chans
    group = freq_group(freqs)
    return pl.pallas_call(
        functools.partial(turn_kernel, half),
        grid=(freqs // group,),
        in_specs=[pl.BlockSpec((group, rows, wide), lambda g: (g, 0, 0))],
        out_specs=pl.BlockSpec((group, chans, double), lambda g: (g, 0, 0)),
        out_shape=jax.ShapeDtypeStruct((freqs, chans, double), jnp.bfloat16),
        scratch_shapes=[pltpu.VMEM((double // LANES, chans, LANES), jnp.float32)] * group,
        compiler_params=pltpu.CompilerParams(vmem_limit_bytes=16 * 2**20),
        cost_estimate=pl.CostEstimate(
            flops=0, bytes_accessed=24 * freqs * chans * double, transcendentals=0
        ),
    )(own)


def freq_group(freqs):
    return max(n for n in range(1, 6) if freqs % n == 0)


def gram_kernel(factor, places, aliased, sel_ref, left_ref, *refs):
    group, chans, _ = left_ref.shape
    found, refs = refs[:places], refs[places + aliased :]
    out_ref, refs = refs[0], refs[1:]
    held, (partners, sems) = refs[:-2], refs[-2:]
    batch = found[0].shape[2] // chans
    reach = chans // batch
    width = batch * chans // LANES
    start = pl.program_id(0) * group

    @pl.when(pl.program_id(0) == 0)
    def _():
        for step in range(STEPS):
            for place, ref in enumerate(found):

                @pl.when(sel_ref[step] == place)
                def _():
                    pltpu.make_async_copy(ref, partners.at[step], sems.at[step]).start()

        for step in range(STEPS):
            pltpu.make_async_copy(found[0], partners.at[step], sems.at[step]).wait()

    for f in range(group):
        left = left_ref[f]
        for step in range(STEPS):
            lines = held[f * STEPS + step]
            packed = partners[step, start + f]
            right = jnp.concatenate(
                [packed[:, r * chans : (r + 1) * chans] for r in range(batch)], axis=0
            )
            empty = jnp.zeros_like(right)
            for part in range(2):
                operand = jnp.concatenate([empty, right] if part else [right, empty], axis=0)
                gram = jnp.dot(left, operand, preferred_element_type=jnp.float32)
                pieces = [gram[r * reach : (r + 1) * reach] for r in range(batch)]
                for m in range(width):
                    parts = []
                    for r in range(batch):
                        low = max(m * LANES - r * chans, 0)
                        high = min((m + 1) * LANES - r * chans, chans)
                        if low < high:
                            parts.append(pieces[r][:, low:high])
                    line = parts[0] if len(parts) == 1 else jnp.concatenate(parts, axis=1)
                    lines[pl.ds(2 * m + part, reach, stride=2 * width), :] = line
            out_ref[step, f] = (lines[...] * factor).astype(jnp.bfloat16)


def cross_stacks(left, found, chosen, factor, total, first, so_far):
    freqs, chans, double = left.shape
    lines = 2 * chans * chans // LANES
    group = freq_group(freqs)
    skip = first // group
    extra = [] if so_far is None else [so_far]
    anywhere = pl.BlockSpec(memory_space=pl.ANY)
    grid_spec = pltpu.PrefetchScalarGridSpec(
        num_scalar_prefetch=1,
        grid=(freqs // group,),
        in_specs=[pl.BlockSpec((group, chans, double), lambda g, sel: (g, 0, 0))]
        + [anywhere] * (len(found) + len(extra)),
        out_specs=pl.BlockSpec((STEPS, group, lines, LANES), lambda g, sel: (0, g + skip, 0, 0)),
        scratch_shapes=[pltpu.VMEM((lines, LANES), jnp.float32)] * (STEPS * group)
        + [
            pltpu.VMEM((STEPS,) + found[0].shape, jnp.bfloat16),
            pltpu.SemaphoreType.DMA((STEPS,)),
        ],
    )
    return pl.pallas_call(
        functools.partial(gram_kernel, factor, len(found), len(extra)),
        grid_spec=grid_spec,
        out_shape=jax.ShapeDtypeStruct((STEPS, total, lines, LANES), jnp.bfloat16),
        input_output_aliases={2 + len(found): 0} if extra else {},
        compiler_params=pltpu.CompilerParams(vmem_limit_bytes=24 * 2**20),
        cost_estimate=pl.CostEstimate(
            flops=4 * STEPS * freqs * double * chans * chans,
            bytes_accessed=12 * STEPS * freqs * chans * chans,
            transcendentals=0,
        ),
    )(chosen, left, *found, *extra)


def fetch_band(own, make_left):
    count = lax.axis_size("chan")
    swap = [(b, b ^ 1) for b in range(count)]
    above = shifted(own, "chan", -2)
    below = shifted(own, "chan", 2)
    twin = lax.ppermute(own, "chan", swap)
    above, below, left = lax.optimization_barrier((above, below, make_left(own)))
    on_down = lax.ppermute(above, "chan", [(b, b - 1) for b in range(2, count, 2)])
    on_up = lax.ppermute(below, "chan", [(b, b + 1) for b in range(1, count - 1, 2)])
    twin_above = lax.ppermute(above, "chan", swap)
    twin_below = lax.ppermute(below, "chan", swap)
    return left, [twin, above, below, twin_above, twin_below, on_down, on_up]


PLACES = ((6, 2, 4, 0, 0, 1, 3), (4, 2, 0, 0, 3, 1, 5))


def per_device(record, valid, pairs):
    channels, seg_len = record.shape
    windows = seg_len // HOP
    samples = record.astype(jnp.float32)
    scale = jnp.sqrt(jnp.mean(samples * samples, axis=-1, keepdims=True) + 1e-05)
    normed = (samples / scale).astype(jnp.bfloat16)
    following = shifted(normed[:, :HOP], "seg", -1)
    extended = jnp.concatenate([normed, following], axis=1)
    frames = jnp.concatenate(
        [
            extended[:, :seg_len].reshape(channels, windows, HOP),
            extended[:, HOP:].reshape(channels, windows, HOP),
        ],
        axis=-1,
    )
    spec = jnp.einsum("cwk,kpf->wpfc", frames, band_table(), preferred_element_type=jnp.float32)
    usable = valid.astype(jnp.float32)
    spectra = (spec * usable[None, None, None, :]).astype(jnp.bfloat16)
    batch = LANES // math.gcd(channels, LANES)
    segs = lax.axis_size("seg")
    freqs = FREQS // segs
    half = windows // batch
    split = spectra.reshape(half, batch, 2, segs, freqs, channels)
    packed = split.transpose(3, 4, 2, 0, 1, 5).reshape(segs, freqs, 2 * half, batch * channels)
    block = lax.axis_index("chan")
    row = jnp.where(block % 2 == 1, jnp.array(PLACES[1]), jnp.array(PLACES[0]))
    chosen = row[pairs[:, 0] - block + BAND].astype(jnp.int32)
    factor = 1.0 / math.sqrt(segs * windows)
    group = freq_group(freqs)
    cut = pl.cdiv(freqs // group, 2) * group
    chunks = []
    for first, last in ((0, cut), (cut, freqs)):
        got = lax.all_to_all(packed[:, first:last], "seg", split_axis=0, concat_axis=0, tiled=True)
        own = got.transpose(1, 0, 2, 3).reshape(last - first, segs * 2 * half, batch * channels)
        chunks.append((first,) + fetch_band(own, lambda x: turned_own(x, channels, half)))
    merged = None
    for first, left, found in chunks:
        merged = cross_stacks(left, found, chosen, factor, freqs, first, merged)
    lines = merged.shape[2]
    merged = merged.reshape(STEPS, freqs, lines // 2, 2, LANES).transpose(0, 3, 1, 2, 4)
    return merged.reshape(STEPS, 2, freqs, channels * channels)


def solution(mesh):
    in_specs = (P("chan", "seg"), P("chan"), P(None, "chan"))
    out_specs = P(None, None, "seg", "chan")
    return jax.shard_map(
        per_device, mesh=mesh, in_specs=in_specs, out_specs=out_specs, check_vma=False
    )
```

```python
import functools
import math

import jax
import jax.numpy as jnp
from jax import lax
from jax.experimental import pallas as pl
from jax.experimental.pallas import tpu as pltpu
from jax.sharding import PartitionSpec as P

FREQS = 200
WIN = 1024
LOW_BIN = 24
STEPS = 2
BAND = 3
HOP = 512
LANES = 128


def shifted(value, axis, steps):
    count = lax.axis_size(axis)
    initial, last = (max(0, -steps), min(count, count - steps))
    return lax.ppermute(value, axis, [(source, source + steps) for source in range(initial, last)])


def band_table():
    steps_k = jnp.arange(WIN, dtype=jnp.int32)
    bins = LOW_BIN + jnp.arange(FREQS, dtype=jnp.int32)
    phase = steps_k[:, None] * bins[None, :] % WIN
    angle = 2.0 * math.pi / WIN * phase.astype(jnp.float32)
    taper = 0.5 - 0.5 * jnp.cos(2.0 * math.pi / WIN * steps_k.astype(jnp.float32))
    factor = (8.0 / (3.0 * WIN)) ** 0.5
    cos_part = taper[:, None] * jnp.cos(angle) * factor
    sin_part = -taper[:, None] * jnp.sin(angle) * factor
    return jnp.stack([cos_part, sin_part], axis=1).astype(jnp.bfloat16)


def turn_kernel(half, own_ref, left_ref, *turns):
    group, rows, wide = own_ref.shape
    chans = left_ref.shape[1]
    batch = wide // chans
    reach = chans // batch
    row = lax.broadcasted_iota(jnp.int32, (rows, chans), 0)
    real = row % (2 * half) < half
    for f in range(group):
        turn = turns[f]
        own = own_ref[f].astype(jnp.float32)
        plain = [own[:, r * chans : (r + 1) * chans] for r in range(batch)]
        turned = [
            jnp.where(real, pltpu.roll(p, rows - half, 0), -pltpu.roll(p, half, 0)) for p in plain
        ]
        upright = jnp.concatenate(plain + turned, axis=0).T
        for k in range(turn.shape[0]):
            turn[k] = upright[:, k * LANES : (k + 1) * LANES]
            for r in range(batch):
                left_ref[f, pl.ds(r * reach, reach), pl.ds(k * LANES, LANES)] = turn[
                    k, pl.ds(r, reach, stride=batch), :
                ].astype(jnp.bfloat16)


def turned_own(own, chans, half):
    freqs, rows, wide = own.shape
    double = 2 * rows * wide // chans
    group = freq_group(freqs)
    return pl.pallas_call(
        functools.partial(turn_kernel, half),
        grid=(freqs // group,),
        in_specs=[pl.BlockSpec((group, rows, wide), lambda g: (g, 0, 0))],
        out_specs=pl.BlockSpec((group, chans, double), lambda g: (g, 0, 0)),
        out_shape=jax.ShapeDtypeStruct((freqs, chans, double), jnp.bfloat16),
        scratch_shapes=[pltpu.VMEM((double // LANES, chans, LANES), jnp.float32)] * group,
        compiler_params=pltpu.CompilerParams(vmem_limit_bytes=16 * 2**20),
        cost_estimate=pl.CostEstimate(
            flops=0, bytes_accessed=24 * freqs * chans * double, transcendentals=0
        ),
    )(own)


def freq_group(freqs):
    return max(n for n in range(1, 6) if freqs % n == 0)


def gram_kernel(factor, places, aliased, sel_ref, left_ref, *refs):
    group, chans, _ = left_ref.shape
    found, refs = refs[:places], refs[places + aliased :]
    out_ref, refs = refs[0], refs[1:]
    held, (partners, sems) = refs[:-2], refs[-2:]
    twin, above, below, theirs, passed = found
    found = [twin, above, below, theirs.at[0], theirs.at[1], passed]
    batch = twin.shape[2] // chans
    reach = chans // batch
    width = batch * chans // LANES
    start = pl.program_id(0) * group

    @pl.when(pl.program_id(0) == 0)
    def _():
        for step in range(STEPS):
            for place, ref in enumerate(found):

                @pl.when(sel_ref[step] == place)
                def _():
                    pltpu.make_async_copy(ref, partners.at[step], sems.at[step]).start()

        for step in range(STEPS):
            pltpu.make_async_copy(found[0], partners.at[step], sems.at[step]).wait()

    for f in range(group):
        left = left_ref[f]
        for step in range(STEPS):
            lines = held[f * STEPS + step]
            packed = partners[step, start + f]
            right = jnp.concatenate(
                [packed[:, r * chans : (r + 1) * chans] for r in range(batch)], axis=0
            )
            empty = jnp.zeros_like(right)
            for part in range(2):
                operand = jnp.concatenate([empty, right] if part else [right, empty], axis=0)
                gram = jnp.dot(left, operand, preferred_element_type=jnp.float32)
                pieces = [gram[r * reach : (r + 1) * reach] for r in range(batch)]
                for m in range(width):
                    parts = []
                    for r in range(batch):
                        low = max(m * LANES - r * chans, 0)
                        high = min((m + 1) * LANES - r * chans, chans)
                        if low < high:
                            parts.append(pieces[r][:, low:high])
                    line = parts[0] if len(parts) == 1 else jnp.concatenate(parts, axis=1)
                    lines[pl.ds(2 * m + part, reach, stride=2 * width), :] = line
            out_ref[step, f] = (lines[...] * factor).astype(jnp.bfloat16)


def cross_stacks(left, found, chosen, factor, total, first, so_far):
    freqs, chans, double = left.shape
    lines = 2 * chans * chans // LANES
    group = freq_group(freqs)
    skip = first // group
    extra = [] if so_far is None else [so_far]
    anywhere = pl.BlockSpec(memory_space=pl.ANY)
    grid_spec = pltpu.PrefetchScalarGridSpec(
        num_scalar_prefetch=1,
        grid=(freqs // group,),
        in_specs=[pl.BlockSpec((group, chans, double), lambda g, sel: (g, 0, 0))]
        + [anywhere] * (len(found) + len(extra)),
        out_specs=pl.BlockSpec((STEPS, group, lines, LANES), lambda g, sel: (0, g + skip, 0, 0)),
        scratch_shapes=[pltpu.VMEM((lines, LANES), jnp.float32)] * (STEPS * group)
        + [
            pltpu.VMEM((STEPS,) + found[0].shape, jnp.bfloat16),
            pltpu.SemaphoreType.DMA((STEPS,)),
        ],
    )
    return pl.pallas_call(
        functools.partial(gram_kernel, factor, len(found), len(extra)),
        grid_spec=grid_spec,
        out_shape=jax.ShapeDtypeStruct((STEPS, total, lines, LANES), jnp.bfloat16),
        input_output_aliases={2 + len(found): 0} if extra else {},
        compiler_params=pltpu.CompilerParams(vmem_limit_bytes=24 * 2**20),
        cost_estimate=pl.CostEstimate(
            flops=4 * STEPS * freqs * double * chans * chans,
            bytes_accessed=12 * STEPS * freqs * chans * chans,
            transcendentals=0,
        ),
    )(chosen, left, *found, *extra)


def fetch_band(own, make_left):
    count = lax.axis_size("chan")
    swap = [(b, b ^ 1) for b in range(count)]
    above = shifted(own, "chan", -2)
    below = shifted(own, "chan", 2)
    twin = lax.ppermute(own, "chan", swap)
    above, below, left = lax.optimization_barrier((above, below, make_left(own)))
    odd = lax.axis_index("chan") % 2 == 1
    forward = [(b, b + 1 if b % 2 else b - 1) for b in range(1, count - 1)]
    passed = lax.ppermute(jnp.where(odd, below, above), "chan", forward)
    theirs = lax.ppermute(jnp.stack([above, below], axis=0), "chan", swap)
    return left, [twin, above, below, theirs, passed]


PLACES = ((5, 2, 4, 0, 0, 1, 3), (4, 2, 0, 0, 3, 1, 5))


def per_device(record, valid, pairs):
    channels, seg_len = record.shape
    windows = seg_len // HOP
    samples = record.astype(jnp.float32)
    scale = jnp.sqrt(jnp.mean(samples * samples, axis=-1, keepdims=True) + 1e-05)
    normed = (samples / scale).astype(jnp.bfloat16)
    following = shifted(normed[:, :HOP], "seg", -1)
    extended = jnp.concatenate([normed, following], axis=1)
    frames = jnp.concatenate(
        [
            extended[:, :seg_len].reshape(channels, windows, HOP),
            extended[:, HOP:].reshape(channels, windows, HOP),
        ],
        axis=-1,
    )
    spec = jnp.einsum("cwk,kpf->wpfc", frames, band_table(), preferred_element_type=jnp.float32)
    usable = valid.astype(jnp.float32)
    spectra = (spec * usable[None, None, None, :]).astype(jnp.bfloat16)
    batch = LANES // math.gcd(channels, LANES)
    segs = lax.axis_size("seg")
    freqs = FREQS // segs
    half = windows // batch
    split = spectra.reshape(half, batch, 2, segs, freqs, channels)
    packed = split.transpose(3, 4, 2, 0, 1, 5).reshape(segs, freqs, 2 * half, batch * channels)
    block = lax.axis_index("chan")
    row = jnp.where(block % 2 == 1, jnp.array(PLACES[1]), jnp.array(PLACES[0]))
    chosen = row[pairs[:, 0] - block + BAND].astype(jnp.int32)
    factor = 1.0 / math.sqrt(segs * windows)
    group = freq_group(freqs)
    cut = pl.cdiv(freqs // group, 2) * group
    chunks = []
    for first, last in ((0, cut), (cut, freqs)):
        got = lax.all_to_all(packed[:, first:last], "seg", split_axis=0, concat_axis=0, tiled=True)
        own = got.transpose(1, 0, 2, 3).reshape(last - first, segs * 2 * half, batch * channels)
        chunks.append((first,) + fetch_band(own, lambda x: turned_own(x, channels, half)))
    merged = None
    for first, left, found in chunks:
        merged = cross_stacks(left, found, chosen, factor, freqs, first, merged)
    lines = merged.shape[2]
    merged = merged.reshape(STEPS, freqs, lines // 2, 2, LANES).transpose(0, 3, 1, 2, 4)
    return merged.reshape(STEPS, 2, freqs, channels * channels)


def solution(mesh):
    in_specs = (P("chan", "seg"), P("chan"), P(None, "chan"))
    out_specs = P(None, None, "seg", "chan")
    return jax.shard_map(
        per_device, mesh=mesh, in_specs=in_specs, out_specs=out_specs, check_vma=False
    )
```

```python
import functools
import math

import jax
import jax.numpy as jnp
from jax import lax
from jax.experimental import pallas as pl
from jax.experimental.pallas import tpu as pltpu
from jax.sharding import PartitionSpec as P

FREQS = 200
WIN = 1024
LOW_BIN = 24
STEPS = 2
BAND = 3
HOP = 512
LANES = 128


def shifted(value, axis, steps):
    count = lax.axis_size(axis)
    initial, last = (max(0, -steps), min(count, count - steps))
    return lax.ppermute(value, axis, [(source, source + steps) for source in range(initial, last)])


def band_table():
    steps_k = jnp.arange(WIN, dtype=jnp.int32)
    bins = LOW_BIN + jnp.arange(FREQS, dtype=jnp.int32)
    phase = steps_k[:, None] * bins[None, :] % WIN
    angle = 2.0 * math.pi / WIN * phase.astype(jnp.float32)
    taper = 0.5 - 0.5 * jnp.cos(2.0 * math.pi / WIN * steps_k.astype(jnp.float32))
    factor = (8.0 / (3.0 * WIN)) ** 0.5
    cos_part = taper[:, None] * jnp.cos(angle) * factor
    sin_part = -taper[:, None] * jnp.sin(angle) * factor
    return jnp.stack([cos_part, sin_part], axis=1).astype(jnp.bfloat16)


def turn_kernel(half, own_ref, left_ref, *turns):
    group, rows, wide = own_ref.shape
    chans = left_ref.shape[1]
    batch = wide // chans
    reach = chans // batch
    row = lax.broadcasted_iota(jnp.int32, (rows, chans), 0)
    real = row % (2 * half) < half
    for f in range(group):
        turn = turns[f]
        own = own_ref[f].astype(jnp.float32)
        plain = [own[:, r * chans : (r + 1) * chans] for r in range(batch)]
        turned = [
            jnp.where(real, pltpu.roll(p, rows - half, 0), -pltpu.roll(p, half, 0)) for p in plain
        ]
        upright = jnp.concatenate(plain + turned, axis=0).T
        for k in range(turn.shape[0]):
            turn[k] = upright[:, k * LANES : (k + 1) * LANES]
            for r in range(batch):
                left_ref[f, pl.ds(r * reach, reach), pl.ds(k * LANES, LANES)] = turn[
                    k, pl.ds(r, reach, stride=batch), :
                ].astype(jnp.bfloat16)


def turned_own(own, chans, half):
    freqs, rows, wide = own.shape
    double = 2 * rows * wide // chans
    group = freq_group(freqs)
    return pl.pallas_call(
        functools.partial(turn_kernel, half),
        grid=(freqs // group,),
        in_specs=[pl.BlockSpec((group, rows, wide), lambda g: (g, 0, 0))],
        out_specs=pl.BlockSpec((group, chans, double), lambda g: (g, 0, 0)),
        out_shape=jax.ShapeDtypeStruct((freqs, chans, double), jnp.bfloat16),
        scratch_shapes=[pltpu.VMEM((double // LANES, chans, LANES), jnp.float32)] * group,
        compiler_params=pltpu.CompilerParams(vmem_limit_bytes=16 * 2**20),
        cost_estimate=pl.CostEstimate(
            flops=0, bytes_accessed=24 * freqs * chans * double, transcendentals=0
        ),
    )(own)


def freq_group(freqs):
    return max(n for n in range(1, 6) if freqs % n == 0)


def gram_kernel(factor, places, aliased, sel_ref, left_ref, *refs):
    group, chans, _ = left_ref.shape
    found, refs = refs[:places], refs[places + aliased :]
    out_ref, refs = refs[0], refs[1:]
    held, (partners, sems) = refs[:-2], refs[-2:]
    batch = found[0].shape[2] // chans
    reach = chans // batch
    width = batch * chans // LANES
    start = pl.program_id(0) * group

    @pl.when(pl.program_id(0) == 0)
    def _():
        for step in range(STEPS):
            for place, ref in enumerate(found):

                @pl.when(sel_ref[step] == place)
                def _():
                    pltpu.make_async_copy(ref, partners.at[step], sems.at[step]).start()

        for step in range(STEPS):
            pltpu.make_async_copy(found[0], partners.at[step], sems.at[step]).wait()

    for f in range(group):
        left = left_ref[f]
        for step in range(STEPS):
            lines = held[f * STEPS + step]
            packed = partners[step, start + f]
            right = jnp.concatenate(
                [packed[:, r * chans : (r + 1) * chans] for r in range(batch)], axis=0
            )
            empty = jnp.zeros_like(right)
            for part in range(2):
                operand = jnp.concatenate([empty, right] if part else [right, empty], axis=0)
                gram = jnp.dot(left, operand, preferred_element_type=jnp.float32)
                pieces = [gram[r * reach : (r + 1) * reach] for r in range(batch)]
                for m in range(width):
                    parts = []
                    for r in range(batch):
                        low = max(m * LANES - r * chans, 0)
                        high = min((m + 1) * LANES - r * chans, chans)
                        if low < high:
                            parts.append(pieces[r][:, low:high])
                    line = parts[0] if len(parts) == 1 else jnp.concatenate(parts, axis=1)
                    lines[pl.ds(2 * m + part, reach, stride=2 * width), :] = line
            out_ref[step, f] = (lines[...] * factor).astype(jnp.bfloat16)


def cross_stacks(left, found, chosen, factor, total, first, so_far):
    freqs, chans, double = left.shape
    lines = 2 * chans * chans // LANES
    group = freq_group(freqs)
    skip = first // group
    extra = [] if so_far is None else [so_far]
    anywhere = pl.BlockSpec(memory_space=pl.ANY)
    grid_spec = pltpu.PrefetchScalarGridSpec(
        num_scalar_prefetch=1,
        grid=(freqs // group,),
        in_specs=[pl.BlockSpec((group, chans, double), lambda g, sel: (g, 0, 0))]
        + [anywhere] * (len(found) + len(extra)),
        out_specs=pl.BlockSpec((STEPS, group, lines, LANES), lambda g, sel: (0, g + skip, 0, 0)),
        scratch_shapes=[pltpu.VMEM((lines, LANES), jnp.float32)] * (STEPS * group)
        + [
            pltpu.VMEM((STEPS,) + found[0].shape, jnp.bfloat16),
            pltpu.SemaphoreType.DMA((STEPS,)),
        ],
    )
    return pl.pallas_call(
        functools.partial(gram_kernel, factor, len(found), len(extra)),
        grid_spec=grid_spec,
        out_shape=jax.ShapeDtypeStruct((STEPS, total, lines, LANES), jnp.bfloat16),
        input_output_aliases={2 + len(found): 0} if extra else {},
        compiler_params=pltpu.CompilerParams(vmem_limit_bytes=24 * 2**20),
        cost_estimate=pl.CostEstimate(
            flops=4 * STEPS * freqs * double * chans * chans,
            bytes_accessed=12 * STEPS * freqs * chans * chans,
            transcendentals=0,
        ),
    )(chosen, left, *found, *extra)


def fetch_band(own, make_left):
    count = lax.axis_size("chan")
    swap = [(b, b ^ 1) for b in range(count)]
    ahead = [1 - 2 * (b % 2) for b in range(count)]
    moves = [[(b + k * ahead[b], b) for b in range(count)] for k in (2, -2, -1)]
    near, far, along = [[(a, b) for a, b in move if 0 <= a < count] for move in moves]
    second = lax.ppermute(own, "chan", near)
    behind = lax.ppermute(own, "chan", far)
    twin = lax.ppermute(own, "chan", swap)
    second, behind, left = lax.optimization_barrier((second, behind, make_left(own)))
    passed = lax.ppermute(second, "chan", along)
    twin_second = lax.ppermute(second, "chan", swap)
    twin_behind = lax.ppermute(behind, "chan", swap)
    return left, [twin, second, behind, twin_second, twin_behind, passed]


PLACES = (5, 2, 3, 0, 0, 1, 4)


def per_device(record, valid, pairs):
    channels, seg_len = record.shape
    windows = seg_len // HOP
    samples = record.astype(jnp.float32)
    scale = jnp.sqrt(jnp.mean(samples * samples, axis=-1, keepdims=True) + 1e-05)
    normed = (samples / scale).astype(jnp.bfloat16)
    following = shifted(normed[:, :HOP], "seg", -1)
    extended = jnp.concatenate([normed, following], axis=1)
    frames = jnp.concatenate(
        [
            extended[:, :seg_len].reshape(channels, windows, HOP),
            extended[:, HOP:].reshape(channels, windows, HOP),
        ],
        axis=-1,
    )
    spec = jnp.einsum("cwk,kpf->wpfc", frames, band_table(), preferred_element_type=jnp.float32)
    usable = valid.astype(jnp.float32)
    spectra = (spec * usable[None, None, None, :]).astype(jnp.bfloat16)
    batch = LANES // math.gcd(channels, LANES)
    segs = lax.axis_size("seg")
    freqs = FREQS // segs
    half = windows // batch
    split = spectra.reshape(half, batch, 2, segs, freqs, channels)
    packed = split.transpose(3, 4, 2, 0, 1, 5).reshape(segs, freqs, 2 * half, batch * channels)
    block = lax.axis_index("chan")
    offset = (pairs[:, 0] - block) * (1 - 2 * (block % 2))
    chosen = jnp.zeros_like(offset)
    for reach_k, place in zip(range(-BAND, BAND + 1), PLACES):
        chosen = jnp.where(offset == reach_k, place, chosen)
    factor = 1.0 / math.sqrt(segs * windows)
    group = freq_group(freqs)
    cut = pl.cdiv(freqs // group, 2) * group
    chunks = []
    for first, last in ((0, cut), (cut, freqs)):
        got = lax.all_to_all(packed[:, first:last], "seg", split_axis=0, concat_axis=0, tiled=True)
        own = got.transpose(1, 0, 2, 3).reshape(last - first, segs * 2 * half, batch * channels)
        chunks.append((first,) + fetch_band(own, lambda x: turned_own(x, channels, half)))
    merged = None
    for first, left, found in chunks:
        merged = cross_stacks(left, found, chosen, factor, freqs, first, merged)
    lines = merged.shape[2]
    merged = merged.reshape(STEPS, freqs, lines // 2, 2, LANES).transpose(0, 3, 1, 2, 4)
    return merged.reshape(STEPS, 2, freqs, channels * channels)


def solution(mesh):
    in_specs = (P("chan", "seg"), P("chan"), P(None, "chan"))
    out_specs = P(None, None, "seg", "chan")
    return jax.shard_map(
        per_device, mesh=mesh, in_specs=in_specs, out_specs=out_specs, check_vma=False
    )
```

```python
import functools
import math

import jax
import jax.numpy as jnp
from jax import lax
from jax.experimental import pallas as pl
from jax.experimental.pallas import tpu as pltpu
from jax.sharding import PartitionSpec as P

FREQS = 200
WIN = 1024
LOW_BIN = 24
STEPS = 2
BAND = 3
HOP = 512
LANES = 128


def shifted(value, axis, steps):
    count = lax.axis_size(axis)
    initial, last = (max(0, -steps), min(count, count - steps))
    return lax.ppermute(value, axis, [(source, source + steps) for source in range(initial, last)])


def band_table():
    steps_k = jnp.arange(WIN, dtype=jnp.int32)
    bins = LOW_BIN + jnp.arange(FREQS, dtype=jnp.int32)
    phase = steps_k[:, None] * bins[None, :] % WIN
    angle = 2.0 * math.pi / WIN * phase.astype(jnp.float32)
    taper = 0.5 - 0.5 * jnp.cos(2.0 * math.pi / WIN * steps_k.astype(jnp.float32))
    factor = (8.0 / (3.0 * WIN)) ** 0.5
    cos_part = taper[:, None] * jnp.cos(angle) * factor
    sin_part = -taper[:, None] * jnp.sin(angle) * factor
    return jnp.stack([cos_part, sin_part], axis=1).astype(jnp.bfloat16)


def turn_kernel(half, own_ref, left_ref, *turns):
    group, rows, wide = own_ref.shape
    chans = left_ref.shape[1]
    batch = wide // chans
    reach = chans // batch
    row = lax.broadcasted_iota(jnp.int32, (rows, chans), 0)
    real = row % (2 * half) < half
    for f in range(group):
        turn = turns[f]
        own = own_ref[f].astype(jnp.float32)
        plain = [own[:, r * chans : (r + 1) * chans] for r in range(batch)]
        turned = [
            jnp.where(real, pltpu.roll(p, rows - half, 0), -pltpu.roll(p, half, 0)) for p in plain
        ]
        upright = jnp.concatenate(plain + turned, axis=0).T
        for k in range(turn.shape[0]):
            turn[k] = upright[:, k * LANES : (k + 1) * LANES]
            for r in range(batch):
                left_ref[f, pl.ds(r * reach, reach), pl.ds(k * LANES, LANES)] = turn[
                    k, pl.ds(r, reach, stride=batch), :
                ].astype(jnp.bfloat16)


def turned_own(own, chans, half):
    freqs, rows, wide = own.shape
    double = 2 * rows * wide // chans
    group = freq_group(freqs)
    return pl.pallas_call(
        functools.partial(turn_kernel, half),
        grid=(freqs // group,),
        in_specs=[pl.BlockSpec((group, rows, wide), lambda g: (g, 0, 0))],
        out_specs=pl.BlockSpec((group, chans, double), lambda g: (g, 0, 0)),
        out_shape=jax.ShapeDtypeStruct((freqs, chans, double), jnp.bfloat16),
        scratch_shapes=[pltpu.VMEM((double // LANES, chans, LANES), jnp.float32)] * group,
        compiler_params=pltpu.CompilerParams(vmem_limit_bytes=16 * 2**20),
        cost_estimate=pl.CostEstimate(
            flops=0, bytes_accessed=24 * freqs * chans * double, transcendentals=0
        ),
    )(own)


def freq_group(freqs):
    return max(n for n in range(1, 6) if freqs % n == 0)


def gram_kernel(factor, places, aliased, sel_ref, left_ref, *refs):
    group, chans, _ = left_ref.shape
    found, refs = refs[:places], refs[places + aliased :]
    out_ref, refs = refs[0], refs[1:]
    held, (partners, sems) = refs[:-2], refs[-2:]
    batch = found[0].shape[2] // chans
    reach = chans // batch
    width = batch * chans // LANES
    start = pl.program_id(0) * group

    @pl.when(pl.program_id(0) == 0)
    def _():
        for step in range(STEPS):
            for place, ref in enumerate(found):

                @pl.when(sel_ref[step] == place)
                def _():
                    pltpu.make_async_copy(ref, partners.at[step], sems.at[step]).start()

        for step in range(STEPS):
            pltpu.make_async_copy(found[0], partners.at[step], sems.at[step]).wait()

    for f in range(group):
        left = left_ref[f]
        for step in range(STEPS):
            lines = held[f * STEPS + step]
            packed = partners[step, start + f]
            right = jnp.concatenate(
                [packed[:, r * chans : (r + 1) * chans] for r in range(batch)], axis=0
            )
            empty = jnp.zeros_like(right)
            for part in range(2):
                operand = jnp.concatenate([empty, right] if part else [right, empty], axis=0)
                gram = jnp.dot(left, operand, preferred_element_type=jnp.float32)
                pieces = [gram[r * reach : (r + 1) * reach] for r in range(batch)]
                for m in range(width):
                    parts = []
                    for r in range(batch):
                        low = max(m * LANES - r * chans, 0)
                        high = min((m + 1) * LANES - r * chans, chans)
                        if low < high:
                            parts.append(pieces[r][:, low:high])
                    line = parts[0] if len(parts) == 1 else jnp.concatenate(parts, axis=1)
                    lines[pl.ds(2 * m + part, reach, stride=2 * width), :] = line
            out_ref[step, f] = (lines[...] * factor).astype(jnp.bfloat16)


def cross_stacks(left, found, chosen, factor, total, first, so_far):
    freqs, chans, double = left.shape
    lines = 2 * chans * chans // LANES
    group = freq_group(freqs)
    skip = first // group
    extra = [] if so_far is None else [so_far]
    anywhere = pl.BlockSpec(memory_space=pl.ANY)
    grid_spec = pltpu.PrefetchScalarGridSpec(
        num_scalar_prefetch=1,
        grid=(freqs // group,),
        in_specs=[pl.BlockSpec((group, chans, double), lambda g, sel: (g, 0, 0))]
        + [anywhere] * (len(found) + len(extra)),
        out_specs=pl.BlockSpec((STEPS, group, lines, LANES), lambda g, sel: (0, g + skip, 0, 0)),
        scratch_shapes=[pltpu.VMEM((lines, LANES), jnp.float32)] * (STEPS * group)
        + [
            pltpu.VMEM((STEPS,) + found[0].shape, jnp.bfloat16),
            pltpu.SemaphoreType.DMA((STEPS,)),
        ],
    )
    return pl.pallas_call(
        functools.partial(gram_kernel, factor, len(found), len(extra)),
        grid_spec=grid_spec,
        out_shape=jax.ShapeDtypeStruct((STEPS, total, lines, LANES), jnp.bfloat16),
        input_output_aliases={2 + len(found): 0} if extra else {},
        compiler_params=pltpu.CompilerParams(vmem_limit_bytes=56 * 2**20),
        cost_estimate=pl.CostEstimate(
            flops=4 * STEPS * freqs * double * chans * chans,
            bytes_accessed=12 * STEPS * freqs * chans * chans,
            transcendentals=0,
        ),
    )(chosen, left, *found, *extra)


def fetch_band(own, make_left):
    count = lax.axis_size("chan")
    swap = [(b, b ^ 1) for b in range(count)]
    ahead = [1 - 2 * (b % 2) for b in range(count)]
    moves = [[(b + k * ahead[b], b) for b in range(count)] for k in (2, -2, -1)]
    near, far, along = [[(a, b) for a, b in move if 0 <= a < count] for move in moves]
    second = lax.ppermute(own, "chan", near)
    behind = lax.ppermute(own, "chan", far)
    twin = lax.ppermute(own, "chan", swap)
    second, behind, left = lax.optimization_barrier((second, behind, make_left(own)))
    passed = lax.ppermute(second, "chan", along)
    twin_second = lax.ppermute(second, "chan", swap)
    twin_behind = lax.ppermute(behind, "chan", swap)
    return left, [twin, second, behind, twin_second, twin_behind, passed]


PLACES = (5, 2, 3, 0, 0, 1, 4)


def per_device(record, valid, pairs):
    channels, seg_len = record.shape
    windows = seg_len // HOP
    samples = record.astype(jnp.float32)
    scale = jnp.sqrt(jnp.mean(samples * samples, axis=-1, keepdims=True) + 1e-05)
    normed = (samples / scale).astype(jnp.bfloat16)
    following = shifted(normed[:, :HOP], "seg", -1)
    extended = jnp.concatenate([normed, following], axis=1)
    frames = jnp.concatenate(
        [
            extended[:, :seg_len].reshape(channels, windows, HOP),
            extended[:, HOP:].reshape(channels, windows, HOP),
        ],
        axis=-1,
    )
    spec = jnp.einsum("cwk,kpf->wpfc", frames, band_table(), preferred_element_type=jnp.float32)
    usable = valid.astype(jnp.float32)
    spectra = (spec * usable[None, None, None, :]).astype(jnp.bfloat16)
    batch = LANES // math.gcd(channels, LANES)
    segs = lax.axis_size("seg")
    freqs = FREQS // segs
    half = windows // batch
    split = spectra.reshape(half, batch, 2, segs, freqs, channels)
    packed = split.transpose(3, 4, 2, 0, 1, 5).reshape(segs, freqs, 2 * half, batch * channels)
    block = lax.axis_index("chan")
    offset = (pairs[:, 0] - block) * (1 - 2 * (block % 2))
    chosen = jnp.zeros_like(offset)
    for reach_k, place in zip(range(-BAND, BAND + 1), PLACES):
        chosen = jnp.where(offset == reach_k, place, chosen)
    factor = 1.0 / math.sqrt(segs * windows)
    group = freq_group(freqs)
    cut = pl.cdiv(freqs // group, 2) * group
    chunks = []
    for first, last in ((0, cut), (cut, freqs)):
        got = lax.all_to_all(packed[:, first:last], "seg", split_axis=0, concat_axis=0, tiled=True)
        own = got.transpose(1, 0, 2, 3).reshape(last - first, segs * 2 * half, batch * channels)
        chunks.append((first,) + fetch_band(own, lambda x: turned_own(x, channels, half)))
    merged = None
    for first, left, found in chunks:
        merged = cross_stacks(left, found, chosen, factor, freqs, first, merged)
    lines = merged.shape[2]
    merged = merged.reshape(STEPS, freqs, lines // 2, 2, LANES).transpose(0, 3, 1, 2, 4)
    return merged.reshape(STEPS, 2, freqs, channels * channels)


def solution(mesh):
    in_specs = (P("chan", "seg"), P("chan"), P(None, "chan"))
    out_specs = P(None, None, "seg", "chan")
    return jax.shard_map(
        per_device, mesh=mesh, in_specs=in_specs, out_specs=out_specs, check_vma=False
    )
```

```python
import functools
import math

import jax
import jax.numpy as jnp
from jax import lax
from jax.experimental import pallas as pl
from jax.experimental.pallas import tpu as pltpu
from jax.sharding import PartitionSpec as P

FREQS = 200
WIN = 1024
LOW_BIN = 24
STEPS = 2
BAND = 3
HOP = 512
LANES = 128


def shifted(value, axis, steps):
    count = lax.axis_size(axis)
    initial, last = (max(0, -steps), min(count, count - steps))
    return lax.ppermute(value, axis, [(source, source + steps) for source in range(initial, last)])


def band_table():
    steps_k = jnp.arange(WIN, dtype=jnp.int32)
    bins = LOW_BIN + jnp.arange(FREQS, dtype=jnp.int32)
    phase = steps_k[:, None] * bins[None, :] % WIN
    angle = 2.0 * math.pi / WIN * phase.astype(jnp.float32)
    taper = 0.5 - 0.5 * jnp.cos(2.0 * math.pi / WIN * steps_k.astype(jnp.float32))
    factor = (8.0 / (3.0 * WIN)) ** 0.5
    cos_part = taper[:, None] * jnp.cos(angle) * factor
    sin_part = -taper[:, None] * jnp.sin(angle) * factor
    return jnp.stack([cos_part, sin_part], axis=1).astype(jnp.bfloat16)


def turn_kernel(half, own_ref, left_ref, *turns):
    group, rows, wide = own_ref.shape
    chans = left_ref.shape[1]
    batch = wide // chans
    reach = chans // batch
    row = lax.broadcasted_iota(jnp.int32, (rows, chans), 0)
    real = row % (2 * half) < half
    for f in range(group):
        turn = turns[f]
        own = own_ref[f].astype(jnp.float32)
        plain = [own[:, r * chans : (r + 1) * chans] for r in range(batch)]
        turned = [
            jnp.where(real, pltpu.roll(p, rows - half, 0), -pltpu.roll(p, half, 0)) for p in plain
        ]
        upright = jnp.concatenate(plain + turned, axis=0).T
        for k in range(turn.shape[0]):
            turn[k] = upright[:, k * LANES : (k + 1) * LANES]
            for r in range(batch):
                left_ref[f, pl.ds(r * reach, reach), pl.ds(k * LANES, LANES)] = turn[
                    k, pl.ds(r, reach, stride=batch), :
                ].astype(jnp.bfloat16)


def turned_own(own, chans, half):
    freqs, rows, wide = own.shape
    double = 2 * rows * wide // chans
    group = freq_group(freqs)
    return pl.pallas_call(
        functools.partial(turn_kernel, half),
        grid=(freqs // group,),
        in_specs=[pl.BlockSpec((group, rows, wide), lambda g: (g, 0, 0))],
        out_specs=pl.BlockSpec((group, chans, double), lambda g: (g, 0, 0)),
        out_shape=jax.ShapeDtypeStruct((freqs, chans, double), jnp.bfloat16),
        scratch_shapes=[pltpu.VMEM((double // LANES, chans, LANES), jnp.float32)] * group,
        compiler_params=pltpu.CompilerParams(vmem_limit_bytes=16 * 2**20),
        cost_estimate=pl.CostEstimate(
            flops=0, bytes_accessed=24 * freqs * chans * double, transcendentals=0
        ),
    )(own)


def freq_group(freqs):
    return max(n for n in range(1, 6) if freqs % n == 0)


def gram_kernel(factor, places, aliased, sel_ref, left_ref, *refs):
    group, chans, _ = left_ref.shape
    found, refs = refs[:places], refs[places + aliased :]
    out_ref, refs = refs[0], refs[1:]
    held, (partners, sems) = refs[:-2], refs[-2:]
    batch = found[0].shape[2] // chans
    reach = chans // batch
    width = batch * chans // LANES
    start = pl.program_id(0) * group

    @pl.when(pl.program_id(0) == 0)
    def _():
        for step in range(STEPS):
            for place, ref in enumerate(found):

                @pl.when(sel_ref[step] == place)
                def _():
                    pltpu.make_async_copy(ref, partners.at[step], sems.at[step]).start()

        for step in range(STEPS):
            pltpu.make_async_copy(found[0], partners.at[step], sems.at[step]).wait()

    for f in range(group):
        left = left_ref[f]
        for step in range(STEPS):
            lines = held[f * STEPS + step]
            packed = partners[step, start + f]
            right = jnp.concatenate(
                [packed[:, r * chans : (r + 1) * chans] for r in range(batch)], axis=0
            )
            empty = jnp.zeros_like(right)
            for part in range(2):
                operand = jnp.concatenate([empty, right] if part else [right, empty], axis=0)
                gram = jnp.dot(left, operand, preferred_element_type=jnp.float32)
                pieces = [gram[r * reach : (r + 1) * reach] for r in range(batch)]
                for m in range(width):
                    parts = []
                    for r in range(batch):
                        low = max(m * LANES - r * chans, 0)
                        high = min((m + 1) * LANES - r * chans, chans)
                        if low < high:
                            parts.append(pieces[r][:, low:high])
                    line = parts[0] if len(parts) == 1 else jnp.concatenate(parts, axis=1)
                    lines[pl.ds(2 * m + part, reach, stride=2 * width), :] = line
            out_ref[step, f] = (lines[...] * factor).astype(jnp.bfloat16)


def cross_stacks(left, found, chosen, factor, total, first, so_far):
    freqs, chans, double = left.shape
    lines = 2 * chans * chans // LANES
    group = freq_group(freqs)
    skip = first // group
    extra = [] if so_far is None else [so_far]
    anywhere = pl.BlockSpec(memory_space=pl.ANY)
    grid_spec = pltpu.PrefetchScalarGridSpec(
        num_scalar_prefetch=1,
        grid=(freqs // group,),
        in_specs=[pl.BlockSpec((group, chans, double), lambda g, sel: (g, 0, 0))]
        + [anywhere] * (len(found) + len(extra)),
        out_specs=pl.BlockSpec((STEPS, group, lines, LANES), lambda g, sel: (0, g + skip, 0, 0)),
        scratch_shapes=[pltpu.VMEM((lines, LANES), jnp.float32)] * (STEPS * group)
        + [
            pltpu.VMEM((STEPS,) + found[0].shape, jnp.bfloat16),
            pltpu.SemaphoreType.DMA((STEPS,)),
        ],
    )
    return pl.pallas_call(
        functools.partial(gram_kernel, factor, len(found), len(extra)),
        grid_spec=grid_spec,
        out_shape=jax.ShapeDtypeStruct((STEPS, total, lines, LANES), jnp.bfloat16),
        input_output_aliases={2 + len(found): 0} if extra else {},
        compiler_params=pltpu.CompilerParams(vmem_limit_bytes=56 * 2**20),
        cost_estimate=pl.CostEstimate(
            flops=4 * STEPS * freqs * double * chans * chans,
            bytes_accessed=12 * STEPS * freqs * chans * chans,
            transcendentals=0,
        ),
    )(chosen, left, *found, *extra)


def fetch_band(own, make_left):
    count = lax.axis_size("chan")
    swap = [(b, b ^ 1) for b in range(count)]
    ahead = [1 - 2 * (b % 2) for b in range(count)]
    moves = [[(b + k * ahead[b], b) for b in range(count)] for k in (2, -2, -1)]
    near, far, along = [[(a, b) for a, b in move if 0 <= a < count] for move in moves]
    second = lax.ppermute(own, "chan", near)
    behind = lax.ppermute(own, "chan", far)
    twin = lax.ppermute(own, "chan", swap)
    second, behind, left = lax.optimization_barrier((second, behind, make_left(own)))
    passed = lax.ppermute(second, "chan", along)
    twin_second = lax.ppermute(second, "chan", swap)
    twin_behind = lax.ppermute(behind, "chan", swap)
    return left, [twin, second, behind, twin_second, twin_behind, passed]


PLACES = (5, 2, 3, 0, 0, 1, 4)


def per_device(record, valid, pairs):
    channels, seg_len = record.shape
    windows = seg_len // HOP
    samples = record.astype(jnp.float32)
    scale = jnp.sqrt(jnp.mean(samples * samples, axis=-1, keepdims=True) + 1e-05)
    normed = (samples / scale).astype(jnp.bfloat16)
    following = shifted(normed[:, :HOP], "seg", -1)
    extended = jnp.concatenate([normed, following], axis=1)
    frames = jnp.concatenate(
        [
            extended[:, :seg_len].reshape(channels, windows, HOP),
            extended[:, HOP:].reshape(channels, windows, HOP),
        ],
        axis=-1,
    )
    spec = jnp.einsum("cwk,kpf->wpfc", frames, band_table(), preferred_element_type=jnp.float32)
    usable = valid.astype(jnp.float32)
    spectra = (spec * usable[None, None, None, :]).astype(jnp.bfloat16)
    batch = LANES // math.gcd(channels, LANES)
    segs = lax.axis_size("seg")
    freqs = FREQS // segs
    half = windows // batch
    split = spectra.reshape(half, batch, 2, segs, freqs, channels)
    packed = split.transpose(3, 4, 2, 0, 1, 5).reshape(segs, freqs, 2 * half, batch * channels)
    block = lax.axis_index("chan")
    offset = (pairs[:, 0] - block) * (1 - 2 * (block % 2))
    chosen = jnp.zeros_like(offset)
    for reach_k, place in zip(range(-BAND, BAND + 1), PLACES):
        chosen = jnp.where(offset == reach_k, place, chosen)
    factor = 1.0 / math.sqrt(segs * windows)
    group = freq_group(freqs)
    cut = max(1, 2 * (freqs // group) // 5) * group
    chunks = []
    for first, last in ((0, cut), (cut, freqs)):
        got = lax.all_to_all(packed[:, first:last], "seg", split_axis=0, concat_axis=0, tiled=True)
        own = got.transpose(1, 0, 2, 3).reshape(last - first, segs * 2 * half, batch * channels)
        chunks.append((first,) + fetch_band(own, lambda x: turned_own(x, channels, half)))
    merged = None
    for first, left, found in chunks:
        merged = cross_stacks(left, found, chosen, factor, freqs, first, merged)
    lines = merged.shape[2]
    merged = merged.reshape(STEPS, freqs, lines // 2, 2, LANES).transpose(0, 3, 1, 2, 4)
    return merged.reshape(STEPS, 2, freqs, channels * channels)


def solution(mesh):
    in_specs = (P("chan", "seg"), P("chan"), P(None, "chan"))
    out_specs = P(None, None, "seg", "chan")
    return jax.shard_map(
        per_device, mesh=mesh, in_specs=in_specs, out_specs=out_specs, check_vma=False
    )
```
